256 devices in a mesh: row: 32 (over y, x, z_hi), col: 8 (over z_lo, core).
Axes of the slice: x: 4, y: 4, z: 8 (z_hi: 2, z_lo: 4; z = z_hi * 4 + z_lo), core: 2. Of those that a mesh axis runs over, the one named last changes fastest.
Arguments:
- green_function: float32 [64, 64, 64, 128], P('row', 'col'), may hold values from -3 to 3
- hamiltonian: float32 [64, 128], replicated, may hold values from -3 to 3
Outputs:
- green_out: float32 [64, 64, 64, 128], P('row', 'col')
The draws below stay inside these ranges and needn't reach their ends.
All inputs are finite; a program needn't handle non-finite values.
Results may differ from the reference program's by a relative error of at most 0.00019.
Values sent between devices are 32-bit elements; how exact they have to be, the bound alone decides.
No kernel may reach another device: no remote copies, remote signals or barrier semaphores. Data moves between devices by JAX's collectives and lax.ppermute only.
A program may use at most 64 MiB of HBM per device.

```python
import jax
import jax.numpy as jnp
from jax import lax

NORB = 64
STEPS = 2
NT = 64


def level_of(rng, shape, pieces, smallest, high):
    gain, own = 1.0, jax.random.fold_in(rng, 6)
    for position, parts in pieces:
        heights = jnp.exp(jax.random.uniform(jax.random.fold_in(own, position), (parts,), jnp.float32, smallest / len(pieces), high / len(pieces)))
        gain = gain * jnp.repeat(heights, shape[position] // parts).reshape([-1 if axis == position else 1 for axis in range(len(shape))])
    return gain


def noise(stream_key, shape, scale, most, shards=(), held_as=jnp.bfloat16):
    factor_of = level_of(stream_key, shape, shards, -0.22, 0.18) if shards else 1.0
    values = jax.random.normal(stream_key, shape, jnp.float32) * scale * factor_of
    return jnp.minimum(jnp.maximum(values, -most), most).astype(held_as)


def setup_inputs(seed: int = 0) -> dict:
    streams_of = jax.random.split(jax.random.key(seed), 3)
    return {
        "green_function": noise(streams_of[0], (NT, NT, NORB, 2 * NORB), 0.5, 3.0, ((0, 32), (1, 8)), jnp.float32),
        "hamiltonian": noise(streams_of[1], (NORB, 2 * NORB), 0.5, 3.0, (), jnp.float32),
    }


time_step = 0.1


def rotate(values):
    half = values.shape[-1] // 2
    return jnp.concatenate([-values[..., half:], values[..., :half]], axis=-1)


def advance(green_function, hamiltonian, weight):
    orbits = green_function.shape[2]
    count = green_function.shape[0]
    real_part = green_function[..., :orbits]
    imag_part = green_function[..., orbits:]
    magnitude = real_part * real_part + imag_part * imag_part
    scaled = jnp.concatenate([magnitude, magnitude], axis=-1) * green_function
    sigma = -(time_step * weight)[:, :, None, None] * scaled
    sigma_pair = jnp.concatenate([-sigma, rotate(sigma)], axis=2)

    def one_row(sigma_row):
        return jnp.einsum("sxq,uskq->ukx", sigma_row, green_function, precision=lax.Precision.HIGHEST)

    partial_value = lax.map(one_row, sigma_pair)
    integral = partial_value.reshape(count, count, orbits, 2, orbits).transpose(0, 1, 4, 3, 2).reshape(count, count, orbits, 2 * orbits)
    ham_real = hamiltonian[:, :orbits]
    ham_imag = hamiltonian[:, orbits:]
    driven = jnp.einsum("ij,tujq->tuiq", ham_real, green_function, precision=lax.Precision.HIGHEST)
    driven = driven + jnp.einsum("ij,tujq->tuiq", ham_imag, rotate(green_function), precision=lax.Precision.HIGHEST)
    driven = driven + integral
    return green_function - time_step * rotate(driven)


def reference(green_function, hamiltonian):
    count = green_function.shape[0]
    times = jnp.arange(count, dtype=jnp.int32)
    first = times[:, None]
    second = times[None, :]
    weight = jnp.where(second < first, jnp.float32(1.0), jnp.where(second == first, jnp.float32(0.5), jnp.float32(0.0)))
    weight = weight.astype(green_function.dtype)
    for repeat in range(STEPS):
        green_function = advance(green_function, hamiltonian, weight)
    return green_function
```

```python
import functools

import jax
import jax.numpy as jnp
from jax import lax
from jax.experimental import pallas as pl
from jax.experimental.pallas import tpu as pltpu
from jax.sharding import Mesh, PartitionSpec as P

STEPS = 2
DT = 0.1
F32, BF16 = jnp.float32, jnp.bfloat16
N = 64
W = 2 * N


def rotate(values):
    lane = lax.broadcasted_iota(jnp.int32, values.shape, values.ndim - 1)
    rolled = pltpu.roll(values, N, values.ndim - 1)
    return jnp.where(lane < N, -rolled, rolled)


def split(values):
    high = values.astype(BF16)
    return high, (values - high.astype(F32)).astype(BF16)


def dot_t(a, b):
    return lax.dot_general(a, b, (((1,), (1,)), ((), ())), preferred_element_type=F32)


def kernel(last, pos, *refs):
    t_refs, own_refs, other_refs = refs[0:4], refs[4:8], refs[8:12]
    ham, out, lhs_hi, lhs_lo, rhs_hi, rhs_lo, stacked = refs[12:]
    y, x, zh, zl, c = (pos[n] for n in range(5))
    zpp = pl.program_id(0)

    def place(value, ypp, j, xp, zp):
        if last:
            out[zp, ypp, xp, 0, j] = value
        else:
            out[0, ypp, j, xp, zp] = value

    @pl.when(zpp == 0)
    def _():
        for k in range(4):
            xp = lax.rem(x - k + 4, 4)
            for zp in range(2):
                t = 16 * y + 4 * xp + 2 * zp + c
                row = (2 * k + zp) * N
                for n in range(8):
                    s = 16 * zl + 4 * (n // 2) + 2 * zh + n % 2
                    weight = jnp.where(s < t, F32(DT * DT), jnp.where(s == t, F32(0.5 * DT * DT), F32(0.0)))
                    g = t_refs[k][zp, n // 2, n % 2]
                    square = g * g
                    scaled = ((square + pltpu.roll(square, N, 1)) * weight) * g
                    high, low = split(scaled)
                    lhs_hi[row:row + N, n * W:(n + 1) * W] = high
                    lhs_lo[row:row + N, n * W:(n + 1) * W] = low

    for k in range(4):
        ypp = lax.rem(y - k + 4, 4)
        for side, ref in ((0, own_refs[k]), (1, other_refs[k])):
            for n in range(8):
                g = ref[0, n // 2, n % 2]
                row = side * W
                col = slice(n * W, (n + 1) * W)
                high, low = split(rotate(g))
                rhs_hi[row:row + N, col] = high
                rhs_lo[row:row + N, col] = low
                high, low = split(-g)
                rhs_hi[row + N:row + W, col] = high
                rhs_lo[row + N:row + W, col] = low
        total = dot_t(lhs_lo[...], rhs_hi[...]) + dot_t(lhs_hi[...], rhs_lo[...]) + dot_t(lhs_hi[...], rhs_hi[...])
        for side in range(2):
            j = c if side == 0 else 1 - c
            for kk in range(4):
                xp = lax.rem(x - kk + 4, 4)
                for zp in range(2):
                    row = (2 * kk + zp) * N
                    place(total[row:row + N, side * W:(side + 1) * W], ypp, j, xp, zp)

    @pl.when(zpp == zh)
    def _():
        for kk in range(4):
            for zp in range(2):
                for j in range(2):
                    n = (2 * kk + zp) * 2 + j
                    g = t_refs[kk][zp, x, j]
                    stacked[:N, n * W:(n + 1) * W] = -rotate(g)
                    stacked[N:, n * W:(n + 1) * W] = g
        turned = DT * lax.dot_general(
            ham[...], stacked[...], (((1,), (0,)), ((), ())),
            preferred_element_type=F32, precision=lax.Precision.HIGHEST,
        )
        for kk in range(4):
            xp = lax.rem(x - kk + 4, 4)
            for zp in range(2):
                for j in range(2):
                    n = (2 * kk + zp) * 2 + j
                    base = stacked[N:, n * W:(n + 1) * W] + turned[:, n * W:(n + 1) * W]
                    if last:
                        out[zp, zl, xp, 0, j] += base
                    else:
                        out[0, zl, j, xp, zp] += base


def partial_sums(last, pos, t_blocks, own_blocks, other_blocks, ham):
    whole = pl.BlockSpec((2, 4, 2, N, W), lambda n, pos: (0, 0, 0, 0, 0))
    half = pl.BlockSpec((1, 4, 2, N, W), lambda n, pos: (n, 0, 0, 0, 0))
    if last:
        shape = (2, 4, 4, 2, 2, N, W)
        out_spec = pl.BlockSpec((2, 4, 4, 1, 2, N, W), lambda n, pos: (0, 0, 0, n, 0, 0, 0))
    else:
        shape = (2, 4, 2, 4, 2, N, W)
        out_spec = pl.BlockSpec((1, 4, 2, 4, 2, N, W), lambda n, pos: (n, 0, 0, 0, 0, 0, 0))
    return pl.pallas_call(
        functools.partial(kernel, last),
        grid_spec=pltpu.PrefetchScalarGridSpec(
            num_scalar_prefetch=1,
            grid=(2,),
            in_specs=[whole] * 4 + [half] * 8 + [pl.BlockSpec((N, W), lambda n, pos: (0, 0))],
            out_specs=out_spec,
            scratch_shapes=[
                pltpu.VMEM((8 * N, 8 * W), BF16),
                pltpu.VMEM((8 * N, 8 * W), BF16),
                pltpu.VMEM((2 * W, 8 * W), BF16),
                pltpu.VMEM((2 * W, 8 * W), BF16),
                pltpu.VMEM((W, 16 * W), F32),
            ],
        ),
        out_shape=jax.ShapeDtypeStruct(shape, F32),
        compiler_params=pltpu.CompilerParams(vmem_limit_bytes=48 * 1024 * 1024),
        name="partial_sums",
    )(pos, *t_blocks, *own_blocks, *other_blocks, ham)


def ring(shift):
    return [(n, (n + shift) % 4) for n in range(4)]


SWAP = [(0, 1), (1, 0)]


def body(green, hamiltonian):
    pos = jnp.stack([lax.axis_index(a) for a in ("y", "x", "zh", "zl", "c")]).astype(jnp.int32)
    block = green.reshape(2, 2, 2, 2, N, W).transpose(2, 0, 1, 3, 4, 5).reshape(4, 2, 2, N, W)
    block = lax.all_to_all(block, ("zh", "c"), 0, 0, tiled=True)
    block = block.reshape(2, 4, 2, N, W)
    for step in range(STEPS):
        last = step == STEPS - 1
        t_blocks = [block] + [lax.ppermute(block, "x", ring(k)) for k in (1, 2, 3)]
        own = [block] + [lax.ppermute(block, "y", ring(k)) for k in (1, 2, 3)]
        other = [lax.ppermute(v, "c", SWAP) for v in own]
        sums = partial_sums(last, pos, t_blocks, own, other, hamiltonian)
        sums = sums.reshape((8,) + sums.shape[2:])
        sums = lax.psum_scatter(sums, ("zh", "zl"), scatter_dimension=0, tiled=True)[0]
        if not last:
            moved = lax.all_to_all(sums.transpose(1, 2, 0, 3, 4), "x", 0, 0, tiled=True)
            block = moved.transpose(1, 0, 2, 3, 4)
        else:
            moved = lax.all_to_all(sums, "x", 0, 0, tiled=True)
            moved = lax.all_to_all(moved.reshape(2, 8, N, W), "c", 0, 0, tiled=True)
    return moved


def solution(mesh):
    fine = Mesh(mesh.devices.reshape(4, 4, 2, 4, 2), ("y", "x", "zh", "zl", "c"))
    spec = P(("y", "x", "zh"), ("zl", "c"), None, None)
    return jax.shard_map(body, mesh=fine, in_specs=(spec, P()), out_specs=spec, check_vma=False)
```

```python
import functools

import jax
import jax.numpy as jnp
from jax import lax
from jax.experimental import pallas as pl
from jax.experimental.pallas import tpu as pltpu
from jax.sharding import Mesh, PartitionSpec as P


STEPS = 2
DT = 0.1
F32, BF16 = jnp.float32, jnp.bfloat16
N = 64
W = 2 * N
HALF = (2, 2, 2, N, W)


def rotate(values):
    lane = lax.broadcasted_iota(jnp.int32, values.shape, values.ndim - 1)
    rolled = pltpu.roll(values, N, values.ndim - 1)
    return jnp.where(lane < N, -rolled, rolled)


def split(values):
    high = values.astype(BF16)
    return high, (values - high.astype(F32)).astype(BF16)


def dot_t(a, b):
    return lax.dot_general(a, b, (((1,), (1,)), ((), ())), preferred_element_type=F32)


def prepare(last, pos, *refs):
    count = 4 if last else 8
    t_refs, own_refs, other_refs = refs[:count], refs[:count // 4] + refs[count:count + 3 * count // 4], refs[7 * count // 4:11 * count // 4]
    ham, lhs_hi, lhs_lo, rhs_hi, rhs_lo, base, stacked = refs[11 * count // 4:]
    y, x, zh, zl, c = (pos[n] for n in range(5))

    def block(group, k, h, m, j):
        return group[k][m, h, j] if last else group[2 * k + h][m, j]

    def fill(group, k, h, row):
        top = pl.ds(pl.multiple_of(row, W), N)
        low_rows = pl.ds(pl.multiple_of(row + N, N), N)
        for n in range(8):
            g = block(group, k, h, n // 2, n % 2)
            col = slice(n * W, (n + 1) * W)
            high, low = split(rotate(g))
            rhs_hi[top, col] = high
            rhs_lo[top, col] = low
            high, low = split(-g)
            rhs_hi[low_rows, col] = high
            rhs_lo[low_rows, col] = low

    def half(h, carry):
        zp = h if last else h ^ zh
        for k in range(4):
            xp = lax.rem(x - k + 4, 4)
            t = 16 * y + 4 * xp + 2 * zp + c
            rows = pl.ds(pl.multiple_of((4 * zp + k) * N, N), N)
            for m in range(4):
                xpp, column = (lax.rem(x - k + m + 4, 4), (m - k) % 4) if last else (m, m)
                for j in range(2):
                    s = 16 * zl + 4 * xpp + 2 * zh + j
                    weight = jnp.where(s < t, F32(DT * DT), jnp.where(s == t, F32(0.5 * DT * DT), F32(0.0)))
                    g = block(t_refs, k, h, m, j)
                    square = g * g
                    scaled = ((square + pltpu.roll(square, N, 1)) * weight) * g
                    high, low = split(scaled)
                    n = 2 * column + j
                    lhs_hi[rows, n * W:(n + 1) * W] = high
                    lhs_lo[rows, n * W:(n + 1) * W] = low
            yp = lax.rem(y - k + 4, 4)
            fill(own_refs, k, h, (4 * yp + 2 * zp + c) * W)
            fill(other_refs, k, h, (4 * yp + 2 * zp + 1 - c) * W)
            for j in range(2):
                n = 2 * k + j
                g = block(t_refs, k, h, k if last else x, j)
                stacked[:N, n * W:(n + 1) * W] = -rotate(g)
                stacked[N:, n * W:(n + 1) * W] = g
        turned = DT * lax.dot_general(
            ham[...], stacked[...], (((1,), (0,)), ((), ())),
            preferred_element_type=F32, precision=lax.Precision.HIGHEST,
        )
        for k in range(4):
            for j in range(2):
                n = 2 * k + j
                base[zp, k, j] = stacked[N:, n * W:(n + 1) * W] + turned[:, n * W:(n + 1) * W]
        return carry

    if last:
        lax.fori_loop(0, 2, half, 0)
    else:
        half(0, 0)
        half(1, 0)


def multiply(last, chunks, pos, lhs_hi, lhs_lo, rhs_hi, rhs_lo, base, *outs):
    zh, zl = pos[2], pos[3]
    z = 4 * zh + zl
    for place, r in enumerate(chunks):
        pair = outs[2 * place:2 * place + 2]
        d = lax.rem(z + r, 8)
        first, yp = d // 4, lax.rem(d, 4)
        if last:
            rows = pl.ds(pl.multiple_of(4 * N * first, 4 * N), 4 * N)
            cols = pl.ds(pl.multiple_of(4 * W * yp, 4 * W), 4 * W)
        else:
            rows = pl.ds(0, 8 * N)
            cols = pl.ds(pl.multiple_of(4 * W * yp + 2 * W * first, 2 * W), 2 * W)
        high, right = lhs_hi[rows, :], rhs_hi[cols, :]
        total = dot_t(lhs_lo[rows, :], right) + dot_t(high, rhs_lo[cols, :]) + dot_t(high, right)
        for h in range(2):
            for k in range(4):
                for j in range(2):
                    if last:
                        value = total[k * N:(k + 1) * N, (2 * h + j) * W:(2 * h + j + 1) * W]
                        if r in (0, 4):
                            value = value + jnp.where(zh == h, F32(1.0), F32(0.0)) * base[first, k, j]
                    else:
                        value = total[(4 * h + k) * N:(4 * h + k + 1) * N, j * W:(j + 1) * W]
                        if r == 0:
                            value = value + base[h, k, j]
                    pair[k // 2][k % 2, h, j] = value


SMEM = pl.BlockSpec(memory_space=pltpu.SMEM)
VMEM = pl.BlockSpec(memory_space=pltpu.VMEM)
PARAMS = pltpu.CompilerParams(vmem_limit_bytes=12 * 1024 * 1024)


def prepared(last, pos, t_blocks, own, other, ham):
    args = [*t_blocks, *own[len(own) // 4:], *other, ham]
    left, right = jax.ShapeDtypeStruct((8 * N, 8 * W), BF16), jax.ShapeDtypeStruct((16 * W, 8 * W), BF16)
    return pl.pallas_call(
        functools.partial(prepare, last),
        in_specs=[SMEM] + [VMEM] * len(args),
        out_specs=[VMEM] * 5,
        scratch_shapes=[pltpu.VMEM((W, 8 * W), F32)],
        out_shape=[left, left, right, right, jax.ShapeDtypeStruct((2, 4, 2, N, W), F32)],
        compiler_params=PARAMS,
        cost_estimate=pl.CostEstimate(flops=1 << 28, bytes_accessed=16 << 20, transcendentals=0),
        name="prepare",
    )(pos, *args)


def partial_sums(last, chunks, pos, operands):
    outs = pl.pallas_call(
        functools.partial(multiply, last, chunks),
        in_specs=[SMEM] + [VMEM] * 5,
        out_specs=[VMEM] * (2 * len(chunks)),
        out_shape=[jax.ShapeDtypeStruct(HALF, F32)] * (2 * len(chunks)),
        compiler_params=PARAMS,
        cost_estimate=pl.CostEstimate(
            flops=len(chunks) * 6 * 8 * N * 2 * W * 8 * W, bytes_accessed=len(chunks) << 20, transcendentals=0
        ),
        name="multiply",
    )(pos, *operands)
    return {r: (outs[2 * n], outs[2 * n + 1]) for n, r in enumerate(chunks)}


def ring(size, shift):
    return [(n, (n + shift) % size) for n in range(size)]


CALLS = ((4,), (3, 5), (2, 6), (1, 7), (0,))
Z = ("zh", "zl")


def swap(value, axes):
    size = 2 ** len(axes)
    return lax.ppermute(value, axes, [(n, size - 1 - n) for n in range(size)])


def first_block(green, zh, c):
    green = green.reshape(2, 2, 2, 2, N, W)

    def part(i, k1):
        rows = lax.dynamic_index_in_dim(green, i, 0, keepdims=False)
        return lax.dynamic_index_in_dim(rows, k1, 1, keepdims=False)

    mine = part(c, zh)
    far = swap(part(c, 1 - zh), ("zh",))
    far_cross = swap(part(1 - c, 1 - zh), ("zh", "c"))
    cross = swap(part(1 - c, zh), ("c",))

    def join(same, flipped):
        return jnp.where(c == 0, jnp.concatenate([same, flipped]), jnp.concatenate([flipped, same]))

    near = join(mine, cross)
    far, far_cross, _ = lax.optimization_barrier((far, far_cross, near))
    return [near, join(far, far_cross)]


def ring_sums(own):
    plus, minus = ring(8, 1), ring(8, 7)
    ahead = lax.ppermute(own[4][0], Z, plus)
    behind = lax.ppermute(own[4][1], Z, minus)
    ahead = jnp.concatenate([ahead + own[3][0], own[3][1]])
    behind = jnp.concatenate([own[5][0], behind + own[5][1]])
    for r in (2, 1):
        ahead = lax.ppermute(ahead, Z, plus) + jnp.concatenate(own[r])
        behind = lax.ppermute(behind, Z, minus) + jnp.concatenate(own[8 - r])
    return lax.ppermute(ahead, Z, plus) + jnp.concatenate(own[0]) + lax.ppermute(behind, Z, minus)


def body(green, hamiltonian):
    y, x, zh, zl, c = (lax.axis_index(a) for a in ("y", "x", "zh", "zl", "c"))
    pos = jnp.stack([y, x, zh, zl, c]).astype(jnp.int32)
    blocks = first_block(green, zh, c)
    for step in range(STEPS):
        last = step == STEPS - 1
        own, t_blocks = {0: blocks}, {0: blocks}
        for k in (2, 1, 3):
            own[k] = [lax.ppermute(v, "y", ring(4, k)) for v in blocks]
        for k in (2, 1, 3):
            t_blocks[k] = [lax.ppermute(v, "x", ring(4, k)) for v in blocks]
        own, t_blocks = ([v for k in range(4) for v in group[k]] for group in (own, t_blocks))
        other = [swap(v, ("c",)) for v in own]
        operands = prepared(last, pos, t_blocks, own, other, hamiltonian)
        sums = {}
        for chunks in CALLS:
            sums.update(partial_sums(last, chunks, pos, operands))
        total = ring_sums(sums)
        total = jnp.stack([total[0]] + [lax.ppermute(total[k], "x", ring(4, -k)) for k in (1, 2, 3)])
        blocks = [total]
    joined = total

    def pair(core):
        first = lax.rem(2 * core - x + 4, 4)
        second = lax.rem(2 * core + 1 - x + 4, 4)
        return jnp.concatenate([
            lax.dynamic_index_in_dim(joined, first, 0), lax.dynamic_index_in_dim(joined, second, 0)
        ]).reshape(8, N, W)

    mine, theirs = pair(c), swap(pair(1 - c), ("c",))
    return jnp.where(c == 0, jnp.stack([mine, theirs]), jnp.stack([theirs, mine]))


def solution(mesh):
    fine = Mesh(mesh.devices.reshape(4, 4, 2, 4, 2), ("y", "x", "zh", "zl", "c"))
    spec = P(("y", "x", "zh"), ("zl", "c"), None, None)
    return jax.shard_map(body, mesh=fine, in_specs=(spec, P()), out_specs=spec, check_vma=False)
```

```python
import functools

import jax
import jax.numpy as jnp
from jax import lax
from jax.experimental import pallas as pl
from jax.experimental.pallas import tpu as pltpu
from jax.sharding import Mesh, PartitionSpec as P


STEPS = 2
DT = 0.1
F32, BF16 = jnp.float32, jnp.bfloat16
N = 64
W = 2 * N
HALF = (2, 2, 2, N, W)


def rotate(values):
    lane = lax.broadcasted_iota(jnp.int32, values.shape, values.ndim - 1)
    rolled = pltpu.roll(values, N, values.ndim - 1)
    return jnp.where(lane < N, -rolled, rolled)


def split(values):
    high = values.astype(BF16)
    return high, (values - high.astype(F32)).astype(BF16)


def dot_t(a, b):
    return lax.dot_general(a, b, (((1,), (1,)), ((), ())), preferred_element_type=F32)


def prepare(pos, *refs):
    t_refs, own_refs, other_refs = refs[0:4], refs[0:1] + refs[4:7], refs[7:11]
    ham, lhs_hi, lhs_lo, rhs_hi, rhs_lo, base, stacked = refs[11:]
    y, x, zh, zl, c = (pos[n] for n in range(5))

    def fill(group, k, h, row):
        top = pl.ds(pl.multiple_of(row, W), N)
        low_rows = pl.ds(pl.multiple_of(row + N, N), N)
        for n in range(8):
            g = group[k][n // 2, h, n % 2]
            col = slice(n * W, (n + 1) * W)
            high, low = split(rotate(g))
            rhs_hi[top, col] = high
            rhs_lo[top, col] = low
            high, low = split(-g)
            rhs_hi[low_rows, col] = high
            rhs_lo[low_rows, col] = low

    def half(h, carry):
        for k in range(4):
            xp = lax.rem(x - k + 4, 4)
            t = 16 * y + 4 * xp + 2 * h + c
            rows = pl.ds(pl.multiple_of((4 * h + k) * N, N), N)
            for m in range(4):
                xpp, column = lax.rem(x - k + m + 4, 4), (m - k) % 4
                for j in range(2):
                    s = 16 * zl + 4 * xpp + 2 * zh + j
                    weight = jnp.where(s < t, F32(DT * DT), jnp.where(s == t, F32(0.5 * DT * DT), F32(0.0)))
                    g = t_refs[k][m, h, j]
                    square = g * g
                    scaled = ((square + pltpu.roll(square, N, 1)) * weight) * g
                    high, low = split(scaled)
                    n = 2 * column + j
                    lhs_hi[rows, n * W:(n + 1) * W] = high
                    lhs_lo[rows, n * W:(n + 1) * W] = low
            yp = lax.rem(y - k + 4, 4)
            fill(own_refs, k, h, (4 * yp + 2 * h + c) * W)
            fill(other_refs, k, h, (4 * yp + 2 * h + 1 - c) * W)
            for j in range(2):
                n = 2 * k + j
                g = t_refs[k][k, h, j]
                stacked[:N, n * W:(n + 1) * W] = -rotate(g)
                stacked[N:, n * W:(n + 1) * W] = g
        turned = DT * lax.dot_general(
            ham[...], stacked[...], (((1,), (0,)), ((), ())),
            preferred_element_type=F32, precision=lax.Precision.HIGHEST,
        )
        for k in range(4):
            for j in range(2):
                n = 2 * k + j
                base[h, k, j] = stacked[N:, n * W:(n + 1) * W] + turned[:, n * W:(n + 1) * W]
        return carry

    lax.fori_loop(0, 2, half, 0)


def multiply(chunks, pos, lhs_hi, lhs_lo, rhs_hi, rhs_lo, base, *outs):
    zh, zl, last = pos[2], pos[3], pos[5]
    z = 4 * zh + zl
    stride = chunks[1] - chunks[0] if len(chunks) > 1 else 0

    def one(last, place, carry):
        r = lax.rem(chunks[0] + place * stride, 8)
        d = lax.rem(z + r, 8)
        first, yp = d // 4, lax.rem(d, 4)
        if last:
            rows = pl.ds(pl.multiple_of(4 * N * first, 4 * N), 4 * N)
            cols = pl.ds(pl.multiple_of(4 * W * yp, 4 * W), 4 * W)
        else:
            rows = pl.ds(0, 8 * N)
            cols = pl.ds(pl.multiple_of(4 * W * yp + 2 * W * first, 2 * W), 2 * W)
        high, right = lhs_hi[rows, :], rhs_hi[cols, :]
        total = dot_t(lhs_lo[rows, :], right) + dot_t(high, rhs_lo[cols, :]) + dot_t(high, right)
        for h in range(2):
            here = ((r == 0) | (r == 4)) & (zh == h) if last else r == 0
            part = jnp.where(here, F32(1.0), F32(0.0))
            for k in range(4):
                for j in range(2):
                    if last:
                        value = total[k * N:(k + 1) * N, (2 * h + j) * W:(2 * h + j + 1) * W]
                    else:
                        value = total[(4 * h + k) * N:(4 * h + k + 1) * N, j * W:(j + 1) * W]
                    if 8 in chunks or (last and 4 in chunks):
                        value = value + part * base[first if last else h, k, j]
                    outs[k // 2][place, k % 2, h, j] = value
        return carry

    for case in (False, True):
        @pl.when(last == int(case))
        def _():
            lax.fori_loop(0, len(chunks), functools.partial(one, case), 0)


SMEM = pl.BlockSpec(memory_space=pltpu.SMEM)
VMEM = pl.BlockSpec(memory_space=pltpu.VMEM)
PARAMS = pltpu.CompilerParams(vmem_limit_bytes=12 * 1024 * 1024)


def prepared(pos, t_blocks, own, other, ham):
    args = [*t_blocks, *own[1:], *other, ham]
    left, right = jax.ShapeDtypeStruct((8 * N, 8 * W), BF16), jax.ShapeDtypeStruct((16 * W, 8 * W), BF16)
    return pl.pallas_call(
        prepare,
        in_specs=[SMEM] + [VMEM] * len(args),
        out_specs=[VMEM] * 5,
        scratch_shapes=[pltpu.VMEM((W, 8 * W), F32)],
        out_shape=[left, left, right, right, jax.ShapeDtypeStruct((2, 4, 2, N, W), F32)],
        compiler_params=PARAMS,
        cost_estimate=pl.CostEstimate(flops=1 << 28, bytes_accessed=16 << 20, transcendentals=0),
        name="prepare",
    )(pos, *args)


def partial_sums(chunks, pos, operands):
    count = len(chunks)
    outs = pl.pallas_call(
        functools.partial(multiply, chunks),
        in_specs=[SMEM] + [VMEM] * 5,
        out_specs=[VMEM] * 2,
        out_shape=[jax.ShapeDtypeStruct((count,) + HALF, F32)] * 2,
        compiler_params=PARAMS,
        cost_estimate=pl.CostEstimate(
            flops=count * 6 * 8 * N * 2 * W * 8 * W, bytes_accessed=count << 20, transcendentals=0
        ),
        name="multiply",
    )(pos, *operands)
    return {r % 8: (outs[0][n], outs[1][n]) for n, r in enumerate(chunks)}


def ring(size, shift):
    return [(n, (n + shift) % size) for n in range(size)]


CALLS = ((4,), (3, 5), (2, 6), (7, 8, 9))
Z = ("zh", "zl")


def swap(value, axes):
    size = 2 ** len(axes)
    return lax.ppermute(value, axes, [(n, size - 1 - n) for n in range(size)])


def first_block(green, x, zh, c):
    green = green.reshape(2, 2, 2, 2, N, W)

    def part(i, k1):
        rows = lax.dynamic_index_in_dim(green, i, 0, keepdims=False)
        return lax.dynamic_index_in_dim(rows, k1, 1, keepdims=False)

    mine = part(c, zh)
    far = swap(part(c, 1 - zh), ("zh",))
    far_cross = swap(part(1 - c, 1 - zh), ("zh", "c"))
    cross = swap(part(1 - c, zh), ("c",))

    def join(same, flipped):
        return jnp.where(c == 0, jnp.concatenate([same, flipped]), jnp.concatenate([flipped, same]))

    near, away = join(mine, cross), join(far, far_cross)
    block = jnp.where(zh == 0, jnp.stack([near, away], axis=1), jnp.stack([away, near], axis=1))
    return lax.dynamic_slice_in_dim(jnp.concatenate([block, block]), x, 4)


def around(block):
    own, others = {0: block}, {0: block}
    for k in (2, 1, 3):
        own[k] = lax.ppermute(block, "y", ring(4, k))
    for k in (2, 1, 3):
        others[k] = lax.ppermute(block, "x", ring(4, k))
    return [own[k] for k in range(4)], [others[k] for k in range(4)]


def ring_sums(own):
    plus, minus = ring(8, 1), ring(8, 7)
    ahead = lax.ppermute(own[4][0], Z, plus)
    behind = lax.ppermute(own[4][1], Z, minus)
    ahead = jnp.concatenate([ahead + own[3][0], own[3][1]])
    behind = jnp.concatenate([own[5][0], behind + own[5][1]])
    for r in (2, 1):
        ahead = lax.ppermute(ahead, Z, plus) + jnp.concatenate(own[r])
        behind = lax.ppermute(behind, Z, minus) + jnp.concatenate(own[8 - r])
    return lax.ppermute(ahead, Z, plus) + jnp.concatenate(own[0]) + lax.ppermute(behind, Z, minus)


def body(green, hamiltonian):
    y, x, zh, zl, c = (lax.axis_index(a) for a in ("y", "x", "zh", "zl", "c"))
    pos = jnp.stack([y, x, zh, zl, c]).astype(jnp.int32)

    def advance(step, block):
        now = jnp.concatenate([pos, (step == STEPS - 1).astype(jnp.int32)[None]])
        own, t_blocks = around(block)
        other = [swap(v, ("c",)) for v in own]
        operands = prepared(now, t_blocks, own, other, hamiltonian)
        sums, turn = {}, now
        for chunks in CALLS:
            part = partial_sums(chunks, turn, operands)
            _, turn = lax.optimization_barrier((part, turn))
            sums.update(part)
        total = ring_sums(sums)
        return jnp.stack([total[0]] + [lax.ppermute(total[k], "x", ring(4, -k)) for k in (1, 2, 3)])

    total = lax.fori_loop(0, STEPS, advance, first_block(green, x, zh, c))
    joined = total

    def pair(core):
        first = lax.rem(2 * core - x + 4, 4)
        second = lax.rem(2 * core + 1 - x + 4, 4)
        return jnp.concatenate([
            lax.dynamic_index_in_dim(joined, first, 0), lax.dynamic_index_in_dim(joined, second, 0)
        ]).reshape(8, N, W)

    mine, theirs = pair(c), swap(pair(1 - c), ("c",))
    return jnp.where(c == 0, jnp.stack([mine, theirs]), jnp.stack([theirs, mine]))


def solution(mesh):
    fine = Mesh(mesh.devices.reshape(4, 4, 2, 4, 2), ("y", "x", "zh", "zl", "c"))
    spec = P(("y", "x", "zh"), ("zl", "c"), None, None)
    return jax.shard_map(body, mesh=fine, in_specs=(spec, P()), out_specs=spec, check_vma=False)
```

```python
import functools

import jax
import jax.numpy as jnp
from jax import lax
from jax.experimental import pallas as pl
from jax.experimental.pallas import tpu as pltpu
from jax.sharding import Mesh, PartitionSpec as P


STEPS = 2
DT = 0.1
F32, BF16 = jnp.float32, jnp.bfloat16
N = 64
W = 2 * N
HALF = (2, 2, 2, N, W)


def rotate(values):
    lane = lax.broadcasted_iota(jnp.int32, values.shape, values.ndim - 1)
    rolled = pltpu.roll(values, N, values.ndim - 1)
    return jnp.where(lane < N, -rolled, rolled)


def split(values):
    high = values.astype(BF16)
    return high, (values - high.astype(F32)).astype(BF16)


def dot_t(a, b):
    return lax.dot_general(a, b, (((1,), (1,)), ((), ())), preferred_element_type=F32)


def dot(a, b):
    return lax.dot_general(a, b, (((1,), (0,)), ((), ())), preferred_element_type=F32)


def prepare(pos, *refs):
    t_refs, own_refs, other_refs = refs[0:4], refs[0:1] + refs[4:7], refs[7:11]
    ham, lhs_hi, lhs_lo, rhs_hi, rhs_lo, base, stack_hi, stack_lo = refs[11:]
    y, x, zh, zl, c = (pos[n] for n in range(5))

    def fill(group, k, h, row):
        top = pl.ds(pl.multiple_of(row, W), N)
        low_rows = pl.ds(pl.multiple_of(row + N, N), N)
        for n in range(8):
            g = group[k][n // 2, h, n % 2]
            col = slice(n * W, (n + 1) * W)
            high, low = split(rotate(g))
            rhs_hi[top, col] = high
            rhs_lo[top, col] = low
            high, low = split(-g)
            rhs_hi[low_rows, col] = high
            rhs_lo[low_rows, col] = low

    def half(h, carry):
        for k in range(4):
            xp = lax.rem(x - k + 4, 4)
            t = 16 * y + 4 * xp + 2 * h + c
            rows = pl.ds(pl.multiple_of((4 * h + k) * N, N), N)
            for m in range(4):
                xpp, column = lax.rem(x - k + m + 4, 4), (m - k) % 4
                for j in range(2):
                    s = 16 * zl + 4 * xpp + 2 * zh + j
                    weight = jnp.where(s < t, F32(DT * DT), jnp.where(s == t, F32(0.5 * DT * DT), F32(0.0)))
                    g = t_refs[k][m, h, j]
                    square = g * g
                    scaled = ((square + pltpu.roll(square, N, 1)) * weight) * g
                    high, low = split(scaled)
                    n = 2 * column + j
                    lhs_hi[rows, n * W:(n + 1) * W] = high
                    lhs_lo[rows, n * W:(n + 1) * W] = low
            yp = lax.rem(y - k + 4, 4)
            fill(own_refs, k, h, (4 * yp + 2 * h + c) * W)
            fill(other_refs, k, h, (4 * yp + 2 * h + 1 - c) * W)
            for j in range(2):
                n = 2 * k + j
                g = t_refs[k][k, h, j]
                col = slice(n * W, (n + 1) * W)
                stack_hi[:N, col], stack_lo[:N, col] = split(-rotate(g))
                stack_hi[N:, col], stack_lo[N:, col] = split(g)
        ham_hi, ham_lo = split(ham[...] * F32(DT))
        turned = dot(ham_lo, stack_hi[...]) + dot(ham_hi, stack_lo[...]) + dot(ham_hi, stack_hi[...])
        for k in range(4):
            for j in range(2):
                n = 2 * k + j
                base[h, k, j] = t_refs[k][k, h, j] + turned[:, n * W:(n + 1) * W]
        return carry

    lax.fori_loop(0, 2, half, 0)


def multiply(chunks, pos, lhs_hi, lhs_lo, rhs_hi, rhs_lo, base, *outs):
    zh, zl, last = pos[2], pos[3], pos[5]
    z = 4 * zh + zl
    stride = chunks[1] - chunks[0] if len(chunks) > 1 else 0

    def one(last, place, carry):
        r = lax.rem(chunks[0] + place * stride, 8)
        d = lax.rem(z + r, 8)
        first, yp = d // 4, lax.rem(d, 4)
        if last:
            rows = pl.ds(pl.multiple_of(4 * N * first, 4 * N), 4 * N)
            cols = pl.ds(pl.multiple_of(4 * W * yp, 4 * W), 4 * W)
        else:
            rows = pl.ds(0, 8 * N)
            cols = pl.ds(pl.multiple_of(4 * W * yp + 2 * W * first, 2 * W), 2 * W)
        high, right = lhs_hi[rows, :], rhs_hi[cols, :]
        total = dot_t(lhs_lo[rows, :], right) + dot_t(high, rhs_lo[cols, :]) + dot_t(high, right)
        for h in range(2):
            here = ((r == 0) | (r == 4)) & (zh == h) if last else r == 0
            part = jnp.where(here, F32(1.0), F32(0.0))
            for k in range(4):
                for j in range(2):
                    if last:
                        value = total[k * N:(k + 1) * N, (2 * h + j) * W:(2 * h + j + 1) * W]
                    else:
                        value = total[(4 * h + k) * N:(4 * h + k + 1) * N, j * W:(j + 1) * W]
                    if 8 in chunks or (last and 4 in chunks):
                        value = value + part * base[first if last else h, k, j]
                    outs[k // 2][place, k % 2, h, j] = value
        return carry

    for case in (False, True):
        @pl.when(last == int(case))
        def _():
            lax.fori_loop(0, len(chunks), functools.partial(one, case), 0)


SMEM = pl.BlockSpec(memory_space=pltpu.SMEM)
VMEM = pl.BlockSpec(memory_space=pltpu.VMEM)
PARAMS = pltpu.CompilerParams(vmem_limit_bytes=12 * 1024 * 1024)


def prepared(pos, t_blocks, own, other, ham):
    args = [*t_blocks, *own[1:], *other, ham]
    left, right = jax.ShapeDtypeStruct((8 * N, 8 * W), BF16), jax.ShapeDtypeStruct((16 * W, 8 * W), BF16)
    return pl.pallas_call(
        prepare,
        in_specs=[SMEM] + [VMEM] * len(args),
        out_specs=[VMEM] * 5,
        scratch_shapes=[pltpu.VMEM((W, 8 * W), BF16)] * 2,
        out_shape=[left, left, right, right, jax.ShapeDtypeStruct((2, 4, 2, N, W), F32)],
        compiler_params=PARAMS,
        cost_estimate=pl.CostEstimate(flops=1 << 28, bytes_accessed=16 << 20, transcendentals=0),
        name="prepare",
    )(pos, *args)


def partial_sums(chunks, pos, operands):
    count = len(chunks)
    outs = pl.pallas_call(
        functools.partial(multiply, chunks),
        in_specs=[SMEM] + [VMEM] * 5,
        out_specs=[VMEM] * 2,
        out_shape=[jax.ShapeDtypeStruct((count,) + HALF, F32)] * 2,
        compiler_params=PARAMS,
        cost_estimate=pl.CostEstimate(
            flops=count * 6 * 8 * N * 2 * W * 8 * W, bytes_accessed=count << 20, transcendentals=0
        ),
        name="multiply",
    )(pos, *operands)
    return {r % 8: (outs[0][n], outs[1][n]) for n, r in enumerate(chunks)}


def ring(size, shift):
    return [(n, (n + shift) % size) for n in range(size)]


Z = ("zh", "zl")


def swap(value, axes):
    size = 2 ** len(axes)
    return lax.ppermute(value, axes, [(n, size - 1 - n) for n in range(size)])


def first_block(green, x, zh, c):
    green = green.reshape(2, 2, 2, 2, N, W)

    def part(i, k1):
        rows = lax.dynamic_index_in_dim(green, i, 0, keepdims=False)
        return lax.dynamic_index_in_dim(rows, k1, 1, keepdims=False)

    mine = part(c, zh)
    far = swap(part(c, 1 - zh), ("zh",))
    far_cross = swap(part(1 - c, 1 - zh), ("zh", "c"))
    cross = swap(part(1 - c, zh), ("c",))

    def join(same, flipped):
        return jnp.where(c == 0, jnp.concatenate([same, flipped]), jnp.concatenate([flipped, same]))

    near, away = join(mine, cross), join(far, far_cross)
    block = jnp.where(zh == 0, jnp.stack([near, away], axis=1), jnp.stack([away, near], axis=1))
    return lax.dynamic_slice_in_dim(jnp.concatenate([block, block]), x, 4)


GATHER = (("y", 1), ("x", 1), ("y", 3), ("x", 3), ("y", 2), ("x", 2))


def around(block):
    got = {"y": [block] * 4, "x": [block] * 4}
    for axis, k in GATHER:
        got[axis][k] = lax.ppermute(block, axis, ring(4, k))
    return got["y"], got["x"]


def ring_sums(part):
    plus, minus = ring(8, 1), ring(8, 7)
    own = part((4,), ())
    own.update(part((3, 5), own[4]))
    a_plus, b_minus = lax.ppermute(own[4][0], Z, plus), lax.ppermute(own[4][1], Z, minus)
    b_plus, a_minus = lax.ppermute(own[3][1], Z, plus), lax.ppermute(own[5][0], Z, minus)
    a_plus, b_minus = a_plus + own[3][0], b_minus + own[5][1]
    own.update(part((2, 6), own[3]))
    own.update(part((7, 8, 9), (own[2], a_plus, b_minus)))
    for r in (2, 1, 0):
        a_plus = lax.ppermute(a_plus, Z, plus) + own[r][0]
        b_minus = lax.ppermute(b_minus, Z, minus)
        b_plus = b_plus + own[r][1]
        if r:
            b_minus = b_minus + own[8 - r][1]
            a_minus = a_minus + own[8 - r][0]
            b_plus = lax.ppermute(b_plus, Z, plus)
            a_minus = lax.ppermute(a_minus, Z, minus)
    return jnp.concatenate([a_plus + a_minus, b_plus + b_minus])


def body(green, hamiltonian):
    y, x, zh, zl, c = (lax.axis_index(a) for a in ("y", "x", "zh", "zl", "c"))
    pos = jnp.stack([y, x, zh, zl, c]).astype(jnp.int32)

    def advance(step, block):
        now = jnp.concatenate([pos, (step == STEPS - 1).astype(jnp.int32)[None]])
        own, t_blocks = around(block)
        other = [swap(v, ("c",)) for v in own]
        operands = prepared(now, t_blocks, own, other, hamiltonian)

        def part(chunks, after):
            turn, _ = lax.optimization_barrier((now, after))
            return partial_sums(chunks, turn, operands)

        total = ring_sums(part)
        return jnp.stack([total[0]] + [lax.ppermute(total[k], "x", ring(4, -k)) for k in (1, 2, 3)])

    total = lax.fori_loop(0, STEPS, advance, first_block(green, x, zh, c))
    joined = total

    def pair(core):
        first = lax.rem(2 * core - x + 4, 4)
        second = lax.rem(2 * core + 1 - x + 4, 4)
        return jnp.concatenate([
            lax.dynamic_index_in_dim(joined, first, 0), lax.dynamic_index_in_dim(joined, second, 0)
        ]).reshape(8, N, W)

    mine, theirs = pair(c), swap(pair(1 - c), ("c",))
    return jnp.where(c == 0, jnp.stack([mine, theirs]), jnp.stack([theirs, mine]))


def solution(mesh):
    fine = Mesh(mesh.devices.reshape(4, 4, 2, 4, 2), ("y", "x", "zh", "zl", "c"))
    spec = P(("y", "x", "zh"), ("zl", "c"), None, None)
    return jax.shard_map(body, mesh=fine, in_specs=(spec, P()), out_specs=spec, check_vma=False)
```
